128 devices in a mesh: cell: 128 (over z, x, y, core).
Axes of the slice: x: 4, y: 4, z: 4, core: 2. Of those that a mesh axis runs over, the one named last changes fastest.
Arguments:
- ocean_fields: float32 [12, 262144], P(None, 'cell'), may hold values from -6 to 6
- grad_coef: float32 [2, 4, 262144], P(None, None, 'cell'), may hold values from -4 to 4
- neighbors: int32 [4, 262144], P(None, 'cell'), may hold values from 0 to 262143, as said below
- task_source: int32 [12288], P('cell'), may hold values from 0 to 2047, as said below
- task_dest: int32 [12288], P('cell'), may hold values from 0 to 511, as said below
- area_weights: float32 [12288, 128, 128], P('cell'), may hold values from 0 to 0.015625
- moment_weights: float32 [12288, 2, 128, 128], P('cell'), may hold values from -0.046875 to 0.046875
Outputs:
- atmos_fields: float32 [12, 65536], P(None, 'cell')
The draws below stay inside these ranges and needn't reach their ends.
Inputs may be any that keep to these rules, and one draw needn't show every extreme that they name: neighbors[k, c] lies within 128 cells of c. `task_source`: ocean block b lies on device b // 16; the 96 tasks of one device read blocks of 96 different devices. `task_dest`: atmosphere block g lies on device g // 4; a task held by device d has its destination either on a device at most 2 away from d (exactly 2 away for some tasks) or on device (d + 128 / 2) mod 128; every device holds some tasks of the latter kind.
All inputs are finite; a program needn't handle non-finite values.
Results may differ from the reference program's by a relative error of at most 0.000071.
Values sent between devices are 32-bit elements; how exact they have to be, the bound alone decides.
A program may use at most 64 MiB of HBM per device.

```python
import jax
import jax.numpy as jnp
from jax import lax

F = 12
BLK = 128
NB = 4
HALF = 2
SB = 16
DB = 4
NSRC = 262144
NDST = 65536
TASK_DEV = 96
NTASK = 12288
N_CELL = 128


def draw_neighbors(key, part):
    cells = jnp.arange(NSRC, dtype=jnp.int32)
    offsets = jax.random.randint(jax.random.fold_in(key, 11), (NB, NSRC), -BLK, BLK + 1)
    return jnp.clip(cells[None, :] + offsets, 0, NSRC - 1).astype(jnp.int32)


def draw_task_source(key, part):
    device_keys = jax.random.split(jax.random.fold_in(key, 21), N_CELL)
    owners = jax.vmap(lambda one_key: jax.random.permutation(one_key, N_CELL)[:TASK_DEV])(device_keys)
    within = jax.random.randint(jax.random.fold_in(key, 22), (N_CELL, TASK_DEV), 0, SB)
    return (owners.astype(jnp.int32) * SB + within).reshape(-1).astype(jnp.int32)


def draw_task_dest(key, part):
    period = 2 * HALF + 1
    phase = jax.random.randint(jax.random.fold_in(key, 31), (), 0, period)
    devices = jnp.arange(N_CELL, dtype=jnp.int32)
    remain = (devices - phase + HALF) % period
    polar = devices - remain + HALF
    target = jnp.where((polar >= 0) & (polar < N_CELL), polar, devices)
    across = (devices + N_CELL // 2) % N_CELL
    coins = jax.random.randint(jax.random.fold_in(key, 32), (N_CELL, TASK_DEV), 0, 3)
    coins = coins.at[:, 0].set(2)
    owners = jnp.where(coins == 1, target[:, None], devices[:, None])
    owners = jnp.where(coins == 2, across[:, None], owners)
    within = jax.random.randint(jax.random.fold_in(key, 33), (N_CELL, TASK_DEV), 0, DB)
    return (owners * DB + within).reshape(-1).astype(jnp.int32)


def shard_levels(stream_key, extent, cuts, smallest, top_value):
    def one(position, shards_of):
        steps = jax.random.uniform(jax.random.fold_in(jax.random.fold_in(stream_key, 6), position), (shards_of,), jnp.float32, smallest / len(cuts), top_value / len(cuts))
        return jnp.repeat(jnp.exp(steps), extent[position] // shards_of).reshape((-1,) + (1,) * (len(extent) - position - 1))

    factor_of = one(*cuts[0])
    for cut in cuts[1:]:
        factor_of = factor_of * one(*cut)
    return factor_of


def scatter_about(own_key, shape, scale, most, shards=(), kind=jnp.bfloat16):
    result = jax.random.normal(own_key, shape, jnp.float32) * scale
    if len(shards) > 0:
        result = shard_levels(own_key, shape, shards, -0.22, 0.18) * result
    return jnp.clip(result, min=-most, max=most).astype(kind)


def setup_inputs(seed: int = 0) -> dict:
    seeds = jax.random.split(jax.random.key(seed), 8)
    return {
        "ocean_fields": scatter_about(seeds[0], (F, NSRC), 1.0, 6.0, ((1, 128),), jnp.float32),
        "grad_coef": scatter_about(seeds[1], (2, NB, NSRC), 0.5, 4.0, ((2, 128),), jnp.float32),
        "neighbors": draw_neighbors(jax.random.fold_in(seeds[7], 71), 0),
        "task_source": draw_task_source(jax.random.fold_in(seeds[7], 71), 0),
        "task_dest": draw_task_dest(jax.random.fold_in(seeds[7], 71), 0),
        "area_weights": jnp.clip(0.015625 * jax.random.uniform(seeds[5], (NTASK, BLK, BLK), jnp.float32) ** shard_levels(seeds[5], (NTASK, BLK, BLK), ((0, 128),), -0.2, 0.2), 0.0, 0.015625),
        "moment_weights": scatter_about(seeds[6], (NTASK, 2, BLK, BLK), (1.0 / BLK), 0.046875, ((0, 128),), jnp.float32),
    }


def reference(ocean_fields, grad_coef, neighbors, task_source, task_dest, area_weights, moment_weights):
    beside_all = ocean_fields[:, neighbors]
    differ = beside_all - ocean_fields[:, None, :]
    slope_east = jnp.sum(grad_coef[0][None] * differ, axis=1)
    slope_north = jnp.sum(grad_coef[1][None] * differ, axis=1)
    rebuilt = jnp.stack([ocean_fields, slope_east, slope_north])
    rebuilt = rebuilt.reshape(3, F, NSRC // BLK, BLK)
    picked = jnp.take(rebuilt, task_source.astype(jnp.int32), axis=2)
    partials = jnp.einsum("fti,tij->tfj", picked[0], area_weights, precision=lax.Precision.HIGHEST)
    partials = partials + jnp.einsum("kfti,tkij->tfj", picked[1:], moment_weights, precision=lax.Precision.HIGHEST)
    summed = jax.ops.segment_sum(partials, task_dest.astype(jnp.int32), num_segments=NDST // BLK)
    return jnp.transpose(summed, (1, 0, 2)).reshape(F, NDST)
```

```python
import jax
import jax.numpy as jnp
from jax import lax
from jax.experimental import pallas as pl
from jax.experimental.pallas import tpu as pltpu
from jax.sharding import PartitionSpec as P

MESH = pl.DeviceIdType.MESH
BLK = 128
ROWS = 16
AXES = 3
SIDE = 4
STRIDES = (32, 8, 2)
SPREAD = 11
NEAR = (-2, -1, 1, 2)
WEIGHT_CHUNKS = 4


def slot_offset(axis, slot):
    first, second, core = slot // 8, (slot // 2) % 4, slot % 2
    offset = [first, second]
    offset.insert(axis, 0)
    return (*offset, core)


def negated(offset):
    return (*((-step) % SIDE for step in offset[:3]), offset[3])


PEERS = []
for _slot in range(1, 32):
    for _axis in range(AXES):
        if slot_offset(_axis, _slot) not in PEERS:
            PEERS.append(slot_offset(_axis, _slot))
PEER_ROW = {offset: row for row, offset in enumerate(PEERS)}
PEER_ROW[(0, 0, 0, 0)] = len(PEERS)
WANT_ROWS = len(PEERS)
WANT_PAD = (WANT_ROWS + 8) // 8 * 8


def kernel(
    ocean,
    coef,
    near_cells,
    source,
    dest,
    area,
    moment,
    out,
    window,
    gather_0,
    gather_1,
    gather_2,
    want,
    own_table,
    mask,
    outgoing,
    arrived,
    total,
    final,
    area_v,
    moment_v,
    want_s,
    own_s,
    weight_sem,
    table_sem,
    want_sems,
    halo_sems,
    spread_send,
    spread_recv,
    block_send,
    block_recv,
    final_send,
    final_recv,
):
    gathers = (gather_0, gather_1, gather_2)
    fields, cells = ocean.shape
    blocks = cells // BLK
    tasks = source.shape[0]
    devices = lax.axis_size("cell")
    me = lax.axis_index("cell")
    place = [(me // stride) % SIDE for stride in STRIDES]
    core = me % 2
    along = [
        [((place[axis] + step) % SIDE) * STRIDES[axis] for step in range(SIDE)] for axis in range(AXES)
    ]
    cores = [core, 1 - core]

    def device_at(offset):
        return along[0][offset[0]] + along[1][offset[1]] + along[2][offset[2]] + cores[offset[3]]

    def index_at(distance):
        return (me + distance + devices) % devices

    weight_copies = []
    step = tasks // WEIGHT_CHUNKS
    for chunk in range(WEIGHT_CHUNKS):
        part = pl.ds(chunk * step, step)
        weight_copies.append(
            pltpu.make_async_copy(area.at[part], area_v.at[part], weight_sem.at[2 * chunk])
        )
        weight_copies.append(
            pltpu.make_async_copy(moment.at[part], moment_v.at[part], weight_sem.at[2 * chunk + 1])
        )
    for copy in weight_copies:
        copy.start()

    barrier = pltpu.get_barrier_semaphore()
    for offset in PEERS:
        pl.semaphore_signal(barrier, inc=1, device_id=(device_at(offset),), device_id_type=MESH)
    for distance in NEAR:
        pl.semaphore_signal(barrier, inc=1, device_id=(index_at(distance),), device_id_type=MESH)

    lanes = lax.broadcasted_iota(jnp.int32, (8, BLK), 1)

    def note(task, tables):
        wanted, reader, slot = tables
        origin = source[task]
        goal = dest[task]
        here = lanes == origin // blocks
        away = (goal // SIDE - me + 2 + devices) % devices
        away = jnp.where(away > 4, 5, away)
        return (
            jnp.where(here, origin % blocks, wanted),
            jnp.where(here, task, reader),
            jnp.where(here, away * SIDE + goal % SIDE, slot),
        )

    empty = jnp.zeros((8, BLK), jnp.int32)
    wanted, reader, slot = lax.fori_loop(0, tasks, note, (empty, empty, empty - 1))
    want[pl.ds(WANT_ROWS, 1), :] = wanted[0:1]
    own_table[0:1, :] = reader[0:1]
    own_table[1:2, :] = slot[0:1]
    table_copy = pltpu.make_async_copy(own_table, own_s, table_sem.at[0])
    table_copy.start()

    for block in range(blocks):
        piece = ocean[:, block * BLK : (block + 1) * BLK]
        window[block + 1, 0:fields, :] = piece
        gather_0[0, block, 0:fields, :] = piece

    def slopes(block):
        first_cell = me * cells + (block - 1) * BLK
        column = pl.ds(pl.multiple_of(block * BLK, BLK), BLK)
        for rows in (slice(0, 8), slice(8, ROWS)):
            left = window[block, rows, :]
            mid = window[block + 1, rows, :]
            right = window[block + 2, rows, :]
            east = jnp.zeros_like(mid)
            north = jnp.zeros_like(mid)
            for k in range(4):
                at = jnp.broadcast_to(near_cells[k : k + 1, column], mid.shape) - first_cell
                lane = at & (BLK - 1)
                which = at >> 7
                picks = [
                    jnp.take_along_axis(x, lane, axis=1, mode="promise_in_bounds")
                    for x in (left, mid, right)
                ]
                beside = jnp.where(which == 0, picks[0], jnp.where(which == 1, picks[1], picks[2]))
                differ = beside - mid
                east += jnp.broadcast_to(coef[0, k : k + 1, column], mid.shape) * differ
                north += jnp.broadcast_to(coef[1, k : k + 1, column], mid.shape) * differ
            gather_1[0, block, rows, :] = east
            gather_2[0, block, rows, :] = north

    def inner(block, carry):
        slopes(block)
        return carry

    lax.fori_loop(1, blocks - 1, inner, 0)

    table_copy.wait()
    slots = lax.broadcasted_iota(jnp.int32, (24, BLK), 0)

    def mark(p, carry):
        mask[p] = jnp.where(slots == own_s[1, p], 1.0, 0.0)
        return carry

    lax.fori_loop(0, devices, mark, 0)
    total[...] = jnp.zeros_like(total)

    pl.semaphore_wait(barrier, len(PEERS) + len(NEAR))

    real = pl.ds(0, fields)
    to_right = pltpu.make_async_remote_copy(
        window.at[blocks, real], window.at[0, real], halo_sems.at[0], halo_sems.at[1],
        device_id=(index_at(1),), device_id_type=MESH,
    )
    to_left = pltpu.make_async_remote_copy(
        window.at[1, real], window.at[blocks + 1, real], halo_sems.at[2], halo_sems.at[3],
        device_id=(index_at(-1),), device_id_type=MESH,
    )
    to_right.start()
    to_left.start()
    for offset in PEERS:
        pltpu.make_async_remote_copy(
            want.at[pl.ds(WANT_ROWS, 1)], want.at[pl.ds(PEER_ROW[offset], 1)], want_sems.at[0], want_sems.at[1],
            device_id=(device_at(offset),), device_id_type=MESH,
        ).start()

    def spread(axis):
        copies = []
        for step in (2, 1, 3):
            offset = [0, 0, 0, 0]
            offset[axis] = step
            copies.append(
                pltpu.make_async_remote_copy(
                    gathers[axis].at[0, :, real], gathers[axis].at[step, :, real],
                    spread_send.at[axis, step], spread_recv.at[axis, step],
                    device_id=(device_at(offset),), device_id_type=MESH,
                )
            )
        return copies

    spreads = [spread(axis) for axis in range(AXES)]
    for copy in spreads[0]:
        copy.start()

    to_right.wait_recv()
    to_left.wait_recv()
    slopes(0)
    slopes(blocks - 1)
    for one, other in zip(spreads[1], spreads[2]):
        one.start()
        other.start()

    all_wants = pl.ds(0, WANT_ROWS)
    pltpu.make_async_copy(want.at[all_wants], want.at[all_wants], want_sems.at[1]).wait()
    want_copy = pltpu.make_async_copy(want, want_s, table_sem.at[1])
    want_copy.start()
    want_copy.wait()

    columns = [
        [me - along[axis][0] + along[axis][(-step) % SIDE] for step in range(SIDE)] for axis in range(AXES)
    ]

    def fill(axis, slot):
        row = PEER_ROW[slot_offset(axis, slot)]
        for step in range(SIDE):
            block = want_s[row, columns[axis][step]]
            piece = gathers[axis][step, block]
            if slot == 0:
                arrived[axis, 0, step] = piece
            else:
                outgoing[axis, slot, step] = piece

    def send(axis, slot):
        return pltpu.make_async_remote_copy(
            outgoing.at[axis, slot, :, real], arrived.at[axis, slot, :, real],
            block_send.at[0], block_recv.at[axis, slot],
            device_id=(device_at(negated(slot_offset(axis, slot))),), device_id_type=MESH,
        )

    for axis in range(AXES):
        for copy in spreads[axis]:
            copy.wait_recv()
    before = []
    for order in range(1, 32):
        slot = (SPREAD * order) % 32
        for axis in range(AXES):
            fill(axis, slot)
        for axis, earlier in before:
            send(axis, earlier).start()
        before = [(axis, slot) for axis in range(AXES)]
    for axis in range(AXES):
        fill(axis, 0)
    for axis, earlier in before:
        send(axis, earlier).start()

    for copy in weight_copies:
        copy.wait()

    def split(x):
        high = x.astype(jnp.bfloat16)
        low = (x - high.astype(jnp.float32)).astype(jnp.bfloat16)
        return high, low

    def products(slot):
        first, second, side = slot // 8, (slot // 2) % 4, slot % 2
        partials = []
        owners = []
        for axis in range(AXES):
            steps = [first, second]
            steps.insert(axis, 0)
            for step in range(SIDE):
                steps[axis] = step
                owner = (core + side) % 2
                for a in range(AXES):
                    shift = -steps[a] if a == axis else steps[a]
                    owner = owner + ((place[a] + shift + SIDE) % SIDE) * STRIDES[a]
                task = own_s[0, owner]
                weight = area_v[task] if axis == 0 else moment_v[task, axis - 1]
                weight = jnp.concatenate(split(weight), axis=1)
                value = jnp.concatenate(split(arrived[axis, slot, step]), axis=0)
                product = jnp.dot(value, weight, preferred_element_type=jnp.float32)
                partials.append(
                    (product[:ROWS, :BLK] + product[ROWS:, :BLK])
                    + (product[:ROWS, BLK:] + product[ROWS:, BLK:])
                )
                owners.append(owner)
        for goal in range(24):
            added = total[goal]
            for owner, partial in zip(owners, partials):
                added += jnp.broadcast_to(mask[owner, goal : goal + 1, :], (ROWS, BLK)) * partial
            total[goal] = added

    products(0)

    def body(order, carry):
        slot = (SPREAD * order) % 32
        for axis in range(AXES):
            pltpu.make_async_copy(
                arrived.at[axis, slot, :, real], arrived.at[axis, slot, :, real], block_recv.at[axis, slot]
            ).wait()
        products(slot)
        return carry

    lax.fori_loop(1, 32, body, 0)

    goals = [index_at(distance) for distance in NEAR] + [index_at(devices // 2)]
    origins = (0, 1, 3, 4, 5)
    finals = [
        pltpu.make_async_remote_copy(
            total.at[pl.ds(SIDE * away, SIDE), real], final.at[number, :, real],
            final_send.at[number], final_recv.at[number],
            device_id=(goal,), device_id_type=MESH,
        )
        for number, (away, goal) in enumerate(zip(origins, goals))
    ]
    for copy in reversed(finals):
        copy.start()
    for copy in finals:
        copy.wait_recv()
    for block in range(SIDE):
        added = total[2 * SIDE + block, 0:fields]
        for number in range(len(finals)):
            added += final[number, block, 0:fields]
        out[:, block * BLK : (block + 1) * BLK] = added

    to_right.wait_send()
    to_left.wait_send()
    pltpu.make_async_copy(want.at[all_wants], want.at[all_wants], want_sems.at[0]).wait()
    for copies in spreads:
        for copy in copies:
            copy.wait_send()
    sent = outgoing.at[:, pl.ds(1, 31), :, real]
    pltpu.make_async_copy(sent, sent, block_send.at[0]).wait()
    for copy in finals:
        copy.wait_send()


def shards(ocean_fields, grad_coef, neighbors, task_source, task_dest, area_weights, moment_weights):
    fields, cells = ocean_fields.shape
    tasks = task_source.shape[0]
    blocks = cells // BLK
    devices = lax.axis_size("cell")
    f32, i32 = jnp.float32, jnp.int32
    vmem = pl.BlockSpec(memory_space=pltpu.VMEM)
    smem = pl.BlockSpec(memory_space=pltpu.SMEM)
    far = pl.BlockSpec(memory_space=pl.ANY)
    dma = pltpu.SemaphoreType.DMA
    gather = pltpu.VMEM((SIDE, blocks, ROWS, BLK), f32)
    return pl.pallas_call(
        kernel,
        out_shape=jax.ShapeDtypeStruct((fields, cells // SIDE), f32),
        in_specs=[vmem, vmem, vmem, smem, smem, far, far],
        out_specs=vmem,
        scratch_shapes=[
            pltpu.VMEM((blocks + 2, ROWS, BLK), f32),
            gather,
            gather,
            gather,
            pltpu.VMEM((WANT_PAD, BLK), i32),
            pltpu.VMEM((8, BLK), i32),
            pltpu.VMEM((devices, 24, BLK), f32),
            pltpu.VMEM((AXES, 32, SIDE, ROWS, BLK), f32),
            pltpu.VMEM((AXES, 32, SIDE, ROWS, BLK), f32),
            pltpu.VMEM((24, ROWS, BLK), f32),
            pltpu.VMEM((5, SIDE, ROWS, BLK), f32),
            pltpu.VMEM((tasks, BLK, BLK), f32),
            pltpu.VMEM((tasks, 2, BLK, BLK), f32),
            pltpu.SMEM((WANT_PAD, BLK), i32),
            pltpu.SMEM((8, BLK), i32),
            dma((2 * WEIGHT_CHUNKS,)),
            dma((2,)),
            dma((2,)),
            dma((4,)),
            dma((AXES, SIDE)),
            dma((AXES, SIDE)),
            dma((1,)),
            dma((AXES, 32)),
            dma((5,)),
            dma((5,)),
        ],
        compiler_params=pltpu.CompilerParams(
            collective_id=0, has_side_effects=True, vmem_limit_bytes=60 << 20
        ),
    )(ocean_fields, grad_coef, neighbors, task_source, task_dest, area_weights, moment_weights)


def solution(mesh):
    placed = (
        P(None, "cell"),
        P(None, None, "cell"),
        P(None, "cell"),
        P("cell"),
        P("cell"),
        P("cell", None, None),
        P("cell", None, None, None),
    )
    return jax.shard_map(
        shards, mesh=mesh, in_specs=placed, out_specs=P(None, "cell"), check_vma=False
    )
```

```python
import jax
import jax.numpy as jnp
from jax import lax
from jax.experimental import pallas as pl
from jax.experimental.pallas import tpu as pltpu
from jax.sharding import PartitionSpec as P

MESH = pl.DeviceIdType.MESH
BLK = 128
ROWS = 16
AXES = 3
SIDE = 4
STRIDES = (32, 8, 2)
SPREAD = 11
NEAR = (-2, -1, 1, 2)
WEIGHT_CHUNKS = 4


def slot_offset(axis, slot):
    first, second, core = slot // 8, (slot // 2) % 4, slot % 2
    offset = [0, 0, 0]
    offset[(axis + 1) % AXES] = first
    offset[(axis + 2) % AXES] = second
    return (*offset, core)


def negated(offset):
    return (*((-step) % SIDE for step in offset[:3]), offset[3])


PEERS = []
for _slot in range(1, 32):
    for _axis in range(AXES):
        if slot_offset(_axis, _slot) not in PEERS:
            PEERS.append(slot_offset(_axis, _slot))
PEER_ROW = {offset: row for row, offset in enumerate(PEERS)}
PEER_ROW[(0, 0, 0, 0)] = len(PEERS)
WANT_ROWS = len(PEERS)
WANT_PAD = (WANT_ROWS + 8) // 8 * 8


def kernel(
    ocean_far,
    coef_far,
    near_far,
    source,
    dest,
    area,
    moment,
    out,
    ocean,
    coef,
    near_cells,
    window,
    own_0,
    own_1,
    own_2,
    line_0,
    line_1,
    line_2,
    want,
    own_table,
    mask,
    outgoing,
    arrived,
    total,
    final,
    area_v,
    moment_v,
    want_s,
    own_s,
    input_sem,
    weight_sem,
    table_sem,
    want_sems,
    halo_sems,
    spread_send,
    spread_recv,
    edge_send,
    edge_recv,
    block_send,
    block_recv,
    final_send,
    final_recv,
):
    owns, lines = (own_0, own_1, own_2), (line_0, line_1, line_2)
    fields, cells = ocean.shape
    blocks = cells // BLK
    tasks = source.shape[0]
    devices = lax.axis_size("cell")
    me = lax.axis_index("cell")
    place = [(me // stride) % SIDE for stride in STRIDES]
    core = me % 2
    along = [
        [((place[axis] + step) % SIDE) * STRIDES[axis] for step in range(SIDE)] for axis in range(AXES)
    ]
    cores = [core, 1 - core]

    def device_at(offset):
        return along[0][offset[0]] + along[1][offset[1]] + along[2][offset[2]] + cores[offset[3]]

    def index_at(distance):
        return (me + distance + devices) % devices

    barrier = pltpu.get_barrier_semaphore()
    for offset in PEERS:
        pl.semaphore_signal(barrier, inc=1, device_id=(device_at(offset),), device_id_type=MESH)
    has_left, has_right = me > 0, me < devices - 1
    corner_left = jnp.logical_and(has_left, me % STRIDES[0] == 0)
    corner_right = jnp.logical_and(has_right, me % STRIDES[0] == STRIDES[0] - 1)

    @pl.when(corner_left)
    def _():
        pl.semaphore_signal(barrier, inc=1, device_id=(index_at(-1),), device_id_type=MESH)

    @pl.when(corner_right)
    def _():
        pl.semaphore_signal(barrier, inc=1, device_id=(index_at(1),), device_id_type=MESH)

    input_copies = [
        pltpu.make_async_copy(ocean_far, ocean, input_sem.at[0]),
        pltpu.make_async_copy(near_far, near_cells, input_sem.at[1]),
        pltpu.make_async_copy(coef_far, coef, input_sem.at[2]),
    ]
    weight_copies = []
    step = tasks // WEIGHT_CHUNKS
    for chunk in range(WEIGHT_CHUNKS):
        part = pl.ds(chunk * step, step)
        weight_copies.append(
            pltpu.make_async_copy(area.at[part], area_v.at[part], weight_sem.at[2 * chunk])
        )
        weight_copies.append(
            pltpu.make_async_copy(moment.at[part], moment_v.at[part], weight_sem.at[2 * chunk + 1])
        )
    for copy in input_copies:
        copy.start()

    lanes = lax.broadcasted_iota(jnp.int32, (8, BLK), 1)

    def note(task, tables):
        wanted, reader, slot = tables
        origin = source[task]
        goal = dest[task]
        here = lanes == origin >> 4
        away = ((goal >> 2) - me + 2 + devices) & (devices - 1)
        away = jnp.minimum(away, 5)
        return (
            jnp.where(here, origin & 15, wanted),
            jnp.where(here, task, reader),
            jnp.where(here, away * SIDE + (goal & 3), slot),
        )

    empty = jnp.zeros((8, BLK), jnp.int32)
    wanted, reader, slot = lax.fori_loop(0, tasks, note, (empty, empty, empty - 1), unroll=8)
    want[pl.ds(WANT_ROWS, 1), :] = wanted[0:1]
    own_table[0:1, :] = reader[0:1]
    own_table[1:2, :] = slot[0:1]
    table_copy = pltpu.make_async_copy(own_table, own_s, table_sem.at[0])
    table_copy.start()

    for copy in input_copies:
        copy.wait()
    for copy in weight_copies:
        copy.start()
    for block in range(blocks):
        piece = ocean[:, block * BLK : (block + 1) * BLK]
        window[block + 1, 0:fields, :] = piece
        own_0[block, 0:fields, :] = piece

    def slopes(block):
        first_cell = me * cells + (block - 1) * BLK
        column = pl.ds(pl.multiple_of(block * BLK, BLK), BLK)
        for rows in (slice(0, 8), slice(8, ROWS)):
            left = window[block, rows, :]
            mid = window[block + 1, rows, :]
            right = window[block + 2, rows, :]
            east = jnp.zeros_like(mid)
            north = jnp.zeros_like(mid)
            for k in range(4):
                at = jnp.broadcast_to(near_cells[k : k + 1, column], mid.shape) - first_cell
                lane = at & (BLK - 1)
                which = at >> 7
                picks = [
                    jnp.take_along_axis(x, lane, axis=1, mode="promise_in_bounds")
                    for x in (left, mid, right)
                ]
                beside = jnp.where(which == 0, picks[0], jnp.where(which == 1, picks[1], picks[2]))
                differ = beside - mid
                east += jnp.broadcast_to(coef[0, k : k + 1, column], mid.shape) * differ
                north += jnp.broadcast_to(coef[1, k : k + 1, column], mid.shape) * differ
            own_1[block, rows, :] = east
            own_2[block, rows, :] = north

    def inner(block, carry):
        slopes(block)
        return carry

    lax.fori_loop(1, blocks - 1, inner, 0, unroll=2)

    real = pl.ds(0, fields)

    def spread(axis, part, send_sem, recv_sem):
        copies = []
        for step in (2, 1, 3):
            offset = [0, 0, 0, 0]
            offset[axis] = step
            copies.append(
                pltpu.make_async_remote_copy(
                    owns[axis].at[part, real], lines[axis].at[step - 1, part, real],
                    send_sem.at[axis, step], recv_sem.at[axis, step],
                    device_id=(device_at(offset),), device_id_type=MESH,
                )
            )
        return copies

    inside = pl.ds(1, blocks - 2)
    spreads = [spread(0, pl.ds(0, blocks), spread_send, spread_recv)] + [
        spread(axis, inside, spread_send, spread_recv) for axis in (1, 2)
    ]

    corners = corner_left.astype(jnp.int32) + corner_right.astype(jnp.int32)
    pl.semaphore_wait(barrier, len(PEERS) + corners)

    to_right = pltpu.make_async_remote_copy(
        window.at[blocks, real], window.at[0, real], halo_sems.at[0], halo_sems.at[1],
        device_id=(index_at(1),), device_id_type=MESH,
    )
    to_left = pltpu.make_async_remote_copy(
        window.at[1, real], window.at[blocks + 1, real], halo_sems.at[2], halo_sems.at[3],
        device_id=(index_at(-1),), device_id_type=MESH,
    )
    pl.when(has_right)(to_right.start)
    pl.when(has_left)(to_left.start)
    for offset in PEERS:
        pltpu.make_async_remote_copy(
            want.at[pl.ds(WANT_ROWS, 1)], want.at[pl.ds(PEER_ROW[offset], 1)], want_sems.at[0], want_sems.at[1],
            device_id=(device_at(offset),), device_id_type=MESH,
        ).start()

    for copies in list(zip(*spreads))[1:]:
        for copy in copies:
            copy.start()

    table_copy.wait()
    slots = lax.broadcasted_iota(jnp.int32, (24, BLK), 0)

    def mark(p, carry):
        mask[p] = jnp.where(slots == own_s[1, p], 1.0, 0.0)
        return carry

    lax.fori_loop(0, devices, mark, 0, unroll=8)
    total[...] = jnp.zeros_like(total)

    pl.when(has_left)(to_right.wait_recv)
    pl.when(has_right)(to_left.wait_recv)
    slopes(0)
    slopes(blocks - 1)
    edges = [
        copy
        for side, block in enumerate((0, blocks - 1))
        for axis in (1, 2)
        for copy in spread(axis, pl.ds(block, 1), edge_send.at[side], edge_recv.at[side])
    ]
    for copy in edges:
        copy.start()

    for copy in next(zip(*spreads)):
        copy.start()

    all_wants = pl.ds(0, WANT_ROWS)
    pltpu.make_async_copy(want.at[all_wants], want.at[all_wants], want_sems.at[1]).wait()
    want_copy = pltpu.make_async_copy(want, want_s, table_sem.at[1])
    want_copy.start()
    want_copy.wait()

    columns = [
        [me - along[axis][0] + along[axis][(-step) % SIDE] for step in range(SIDE)] for axis in range(AXES)
    ]

    def fill(axis, slot, steps):
        row = PEER_ROW[slot_offset(axis, slot)]
        for step in steps:
            block = want_s[row, columns[axis][step]]
            piece = lines[axis][step - 1, block] if step else owns[axis][block]
            if slot == 0:
                arrived[axis, 0, step] = piece
            else:
                outgoing[axis, slot, step] = piece

    def send(axis, slot, steps):
        part = pl.ds(steps.start, len(steps))
        return pltpu.make_async_remote_copy(
            outgoing.at[axis, slot, part, real], arrived.at[axis, slot, part, real],
            block_send.at[0], block_recv.at[axis, slot],
            device_id=(device_at(negated(slot_offset(axis, slot))),), device_id_type=MESH,
        )

    def serve(steps):
        before = []
        for order in range(1, 32):
            slot = (SPREAD * order) % 32
            for axis in range(AXES):
                fill(axis, slot, steps)
            for axis, earlier in before:
                send(axis, earlier, steps).start()
            before = [(axis, slot) for axis in range(AXES)]
        for axis in range(AXES):
            fill(axis, 0, steps)
        for axis, earlier in before:
            send(axis, earlier, steps).start()

    serve(range(1))
    for copy in sum(spreads, edges):
        copy.wait_recv()
    serve(range(1, SIDE))

    for copy in weight_copies:
        copy.wait()

    def split(x):
        high = x.astype(jnp.bfloat16)
        low = (x - high.astype(jnp.float32)).astype(jnp.bfloat16)
        return high, low

    def products(slot):
        first, second, side = slot // 8, (slot // 2) % 4, slot % 2
        partials = []
        owners = []
        for axis in range(AXES):
            for step in range(SIDE):
                steps = [step] * AXES
                steps[(axis + 1) % AXES] = first
                steps[(axis + 2) % AXES] = second
                owner = (core + side) % 2
                for a in range(AXES):
                    shift = -steps[a] if a == axis else steps[a]
                    owner = owner + ((place[a] + shift + SIDE) % SIDE) * STRIDES[a]
                task = own_s[0, owner]
                weight = area_v[task] if axis == 0 else moment_v[task, axis - 1]
                weight = jnp.concatenate(split(weight), axis=1)
                value = jnp.concatenate(split(arrived[axis, slot, step]), axis=0)
                product = jnp.dot(value, weight, preferred_element_type=jnp.float32)
                partials.append(
                    (product[:ROWS, :BLK] + product[ROWS:, :BLK])
                    + (product[:ROWS, BLK:] + product[ROWS:, BLK:])
                )
                owners.append(owner)
        for goal in range(24):
            added = total[goal]
            for owner, partial in zip(owners, partials):
                added += jnp.broadcast_to(mask[owner, goal : goal + 1, :], (ROWS, BLK)) * partial
            total[goal] = added

    products(0)

    def body(order, carry):
        slot = (SPREAD * order) % 32
        for axis in range(AXES):
            pltpu.make_async_copy(
                arrived.at[axis, slot, :, real], arrived.at[axis, slot, :, real], block_recv.at[axis, slot]
            ).wait()
        products(slot)
        return carry

    lax.fori_loop(1, 32, body, 0)

    goals = [index_at(distance) for distance in NEAR] + [index_at(devices // 2)]
    origins = (0, 1, 3, 4, 5)
    finals = [
        pltpu.make_async_remote_copy(
            total.at[pl.ds(SIDE * away, SIDE), real], final.at[number, :, real],
            final_send.at[number], final_recv.at[number],
            device_id=(goal,), device_id_type=MESH,
        )
        for number, (away, goal) in enumerate(zip(origins, goals))
    ]
    for copy in reversed(finals):
        copy.start()
    for copy in finals:
        copy.wait_recv()
    for block in range(SIDE):
        added = total[2 * SIDE + block, 0:fields]
        for number in range(len(finals)):
            added += final[number, block, 0:fields]
        out[:, block * BLK : (block + 1) * BLK] = added

    pl.when(has_right)(to_right.wait_send)
    pl.when(has_left)(to_left.wait_send)
    pltpu.make_async_copy(want.at[all_wants], want.at[all_wants], want_sems.at[0]).wait()
    for copy in sum(spreads, edges):
        copy.wait_send()
    sent = outgoing.at[:, pl.ds(1, 31), :, real]
    pltpu.make_async_copy(sent, sent, block_send.at[0]).wait()
    for copy in finals:
        copy.wait_send()


def shards(ocean_fields, grad_coef, neighbors, task_source, task_dest, area_weights, moment_weights):
    fields, cells = ocean_fields.shape
    tasks = task_source.shape[0]
    blocks = cells // BLK
    devices = lax.axis_size("cell")
    f32, i32 = jnp.float32, jnp.int32
    vmem = pl.BlockSpec(memory_space=pltpu.VMEM)
    smem = pl.BlockSpec(memory_space=pltpu.SMEM)
    far = pl.BlockSpec(memory_space=pl.ANY)
    dma = pltpu.SemaphoreType.DMA
    own = pltpu.VMEM((blocks, ROWS, BLK), f32)
    line = pltpu.VMEM((SIDE - 1, blocks, ROWS, BLK), f32)
    return pl.pallas_call(
        kernel,
        out_shape=pltpu.VMEM((fields, cells // SIDE), f32),
        in_specs=[far, far, far, smem, smem, far, far],
        out_specs=vmem,
        scratch_shapes=[
            pltpu.VMEM(ocean_fields.shape, f32),
            pltpu.VMEM(grad_coef.shape, f32),
            pltpu.VMEM(neighbors.shape, i32),
            pltpu.VMEM((blocks + 2, ROWS, BLK), f32),
            own,
            own,
            own,
            line,
            line,
            line,
            pltpu.VMEM((WANT_PAD, BLK), i32),
            pltpu.VMEM((8, BLK), i32),
            pltpu.VMEM((devices, 24, BLK), f32),
            pltpu.VMEM((AXES, 32, SIDE, ROWS, BLK), f32),
            pltpu.VMEM((AXES, 32, SIDE, ROWS, BLK), f32),
            pltpu.VMEM((24, ROWS, BLK), f32),
            pltpu.VMEM((5, SIDE, ROWS, BLK), f32),
            pltpu.VMEM((tasks, BLK, BLK), f32),
            pltpu.VMEM((tasks, 2, BLK, BLK), f32),
            pltpu.SMEM((WANT_PAD, BLK), i32),
            pltpu.SMEM((8, BLK), i32),
            dma((3,)),
            dma((2 * WEIGHT_CHUNKS,)),
            dma((2,)),
            dma((2,)),
            dma((4,)),
            dma((AXES, SIDE)),
            dma((AXES, SIDE)),
            dma((2, AXES, SIDE)),
            dma((2, AXES, SIDE)),
            dma((1,)),
            dma((AXES, 32)),
            dma((5,)),
            dma((5,)),
        ],
        compiler_params=pltpu.CompilerParams(
            collective_id=0, has_side_effects=True, vmem_limit_bytes=60 << 20
        ),
    )(ocean_fields, grad_coef, neighbors, task_source, task_dest, area_weights, moment_weights)


def solution(mesh):
    placed = (
        P(None, "cell"),
        P(None, None, "cell"),
        P(None, "cell"),
        P("cell"),
        P("cell"),
        P("cell", None, None),
        P("cell", None, None, None),
    )
    return jax.shard_map(
        shards, mesh=mesh, in_specs=placed, out_specs=P(None, "cell"), check_vma=False
    )
```
